1024 devices in a mesh: dp: 16 (over y, z_hi, core), mp: 64 (over z_lo, x).
Axes of the slice: x: 4, y: 4, z: 32 (z_hi: 2, z_lo: 16; z = z_hi * 16 + z_lo), core: 2. Of those that a mesh axis runs over, the one named last changes fastest.
Arguments:
- activations: bfloat16 [4096, 8192], P('dp', 'mp'), may hold values from -40 to 40
- out_grads: bfloat16 [4096, 8192], P('dp', 'mp'), may hold values from -40 to 40
- basis_in: bfloat16 [8192, 8192], P(None, 'mp'), may hold values from -1 to 1
- basis_out: bfloat16 [8192, 8192], P(None, 'mp'), may hold values from -1 to 1
- grad_eigen: bfloat16 [8192, 8192], P('mp', 'dp'), may hold values from -8 to 8
Outputs:
- precond: bfloat16 [8192, 8192], P(('mp', 'dp'))
The draws below stay inside these ranges and needn't reach their ends.
All inputs are finite; a program needn't handle non-finite values.
Results may differ from the reference program's by a relative error of at most 0.015.
Values may be sent and summed in bfloat16 or wider, within the bound.
No kernel may reach another device: no remote copies, remote signals or barrier semaphores. Data moves between devices by JAX's collectives and lax.ppermute only.
A program may use at most 32 MiB of HBM per device.

```python
import jax
import jax.numpy as jnp
from jax import lax

D = 8192
TOK_DEV = 256
TOKENS = 4096
N_DP = 16


def basis_draw(key, salt_value):
    key_basis = jax.random.fold_in(key, salt_value)
    values = jnp.clip(jax.random.normal(key_basis, (D, D), jnp.float32), -4.0, 4.0) * D ** (-0.5)
    return values.astype(jnp.bfloat16)


def drawn_rows(key, salt_basis, salt_own, coef_scale, rising):
    basis_full = basis_draw(key, salt_basis).astype(jnp.float32)
    key_own = jax.random.fold_in(key, salt_own)
    key_blocks = jax.random.fold_in(key_own, 3)
    key_values = jax.random.fold_in(key_own, 7)
    key_rows = jax.random.fold_in(key_own, 13)
    token_block = jax.random.randint(key_blocks, (TOKENS, 1), 0, 16)
    column_block = (jnp.arange(D) // (D // 16)).reshape(1, D)
    jitter = jnp.clip(jax.random.normal(key_values, (TOKENS, D), jnp.float32), -4.0, 4.0)
    inside = (column_block == token_block).astype(jnp.float32)
    row_scale = 2.0 ** (jax.random.uniform(key_rows, (TOKENS, 1), jnp.float32) - 0.5)
    if rising:
        position = jnp.arange(TOKENS, dtype=jnp.float32).reshape(TOKENS, 1) / TOKENS
        row_scale = row_scale * 3.0 ** position
    coefficients = jitter * inside * coef_scale * row_scale
    aligned = jnp.dot(coefficients, basis_full.T, precision=lax.Precision.HIGHEST)
    return jnp.clip(aligned, -40.0, 40.0).astype(jnp.bfloat16)


def draw_basis_in(key, part):
    return basis_draw(key, 101)


def draw_basis_out(key, part):
    return basis_draw(key, 202)


def draw_activations(key, part):
    return drawn_rows(key, 101, 303, 2.0, True)


def draw_out_grads(key, part):
    return drawn_rows(key, 202, 404, 3.0, False)


def steps_of(own_key, shape, shards, low, top_value):
    factor_of = 1.0
    for axis_at, parts in shards:
        steps = jax.random.uniform(jax.random.fold_in(jax.random.fold_in(own_key, 6), axis_at), (parts,), jnp.float32, low / len(shards), top_value / len(shards))
        factor_of = factor_of * jnp.repeat(jnp.exp(steps), shape[axis_at] // parts).reshape((-1,) + (1,) * (len(shape) - 1 - axis_at))
    return factor_of


def noise(rng, extent, deviation, limit, split=(), kind=jnp.bfloat16):
    values = deviation * jax.random.normal(rng, extent, jnp.float32)
    if split:
        values = values * steps_of(rng, extent, split, -0.22, 0.18)
    return jnp.clip(values, -limit, limit).astype(kind)


def setup_inputs(seed: int = 0) -> dict:
    seeds = jax.random.split(jax.random.key(seed), 6)
    activations = draw_activations(jax.random.fold_in(seeds[5], 71), 0)
    out_grads = draw_out_grads(jax.random.fold_in(seeds[5], 71), 0)
    basis_in = draw_basis_in(jax.random.fold_in(seeds[5], 71), 0)
    basis_out = draw_basis_out(jax.random.fold_in(seeds[5], 71), 0)
    grad_eigen = noise(seeds[4], (D, D), 2.0, 8.0, ((0, 64), (1, 16)))
    return dict(activations=activations, out_grads=out_grads, basis_in=basis_in, basis_out=basis_out, grad_eigen=grad_eigen)


damping = 0.1


def reference(activations, out_grads, basis_in, basis_out, grad_eigen):
    proj_in = jnp.dot(activations, basis_in, preferred_element_type=jnp.float32)
    squares_in = (proj_in * proj_in).astype(jnp.bfloat16)
    proj_out = jnp.dot(out_grads, basis_out, preferred_element_type=jnp.float32)
    squares_out = (proj_out * proj_out).astype(jnp.bfloat16)
    groups_in = squares_in.reshape(N_DP, TOK_DEV, D)
    groups_out = squares_out.reshape(N_DP, TOK_DEV, D)

    def accumulate(summed, operands):
        left_rows, right_rows = operands
        partial_value = lax.dot_general(left_rows, right_rows, (((0,), (0,)), ((), ())), preferred_element_type=jnp.float32)
        partial_value = lax.optimization_barrier(partial_value.astype(jnp.bfloat16)).astype(jnp.float32)
        return summed + partial_value, None

    summed, unused = lax.scan(accumulate, jnp.zeros((D, D), jnp.float32), (groups_in, groups_out))
    scaling = summed / (TOK_DEV * N_DP)
    return (grad_eigen.astype(jnp.float32) / (scaling + damping)).astype(jnp.bfloat16)
```

```python
import jax
import jax.numpy as jnp
from jax import lax
from jax.sharding import Mesh, PartitionSpec as P

damping = 0.1
Y, ZH, C, X = 4, 2, 2, 4
Z_BITS = ("z8", "z4", "z2", "z1")
AXES = ("y", "zh", "c") + Z_BITS + ("x",)
f32, bf16 = jnp.float32, jnp.bfloat16


def swap(value, axis):
    return lax.ppermute(value, axis, [(0, 1), (1, 0)])


def gather_z(block):
    have = block[None]
    for axis in Z_BITS:
        other = swap(have, axis)
        upper = lax.axis_index(axis) == 1
        low = jnp.where(upper, other, have)
        high = jnp.where(upper, have, other)
        have = jnp.stack([low, high], axis=1).reshape((-1,) + block.shape)
    return have


def basis_over_x(basis):
    blocks = basis.reshape(16, X, 128, 128)
    return lax.all_to_all(blocks, "x", split_axis=1, concat_axis=1, tiled=True)


def add_over(value, axis):
    parts = lax.all_to_all(value, axis, split_axis=0, concat_axis=0, tiled=True)
    return jnp.sum(parts.astype(f32), axis=0)


def per_device(activations, out_grads, basis_in, basis_out, grad_eigen):
    tokens = activations.shape[0]
    z_out = gather_z(out_grads)
    z_in = gather_z(activations)
    b_out = basis_over_x(basis_out)
    b_in = basis_over_x(basis_in)

    part_out = jnp.einsum("ztf,zxfc->xtc", z_out, b_out, preferred_element_type=f32)
    proj_out = add_over(part_out.astype(bf16), "x")
    squares_out = (proj_out * proj_out).astype(bf16)
    z_squares = gather_z(squares_out)

    part_in = jnp.einsum("zxfc,ztf->xct", b_in, z_in, preferred_element_type=f32)
    proj_in = add_over(part_in.astype(bf16), "x")
    squares_in = (proj_in * proj_in).astype(bf16)
    rows_in = lax.all_gather(squares_in, "x", axis=0, tiled=False)
    rows_in = rows_in.reshape(X, Y, ZH, C, 8, tokens)
    rows_in = rows_in.transpose(3, 1, 2, 0, 4, 5).reshape(C * Y * ZH * X * 8, tokens)

    partial = jnp.einsum("rt,ztc->rzc", rows_in, z_squares, preferred_element_type=f32)
    partial = partial.reshape(C, Y * ZH * X * 8, 2048).astype(bf16)
    partial = add_over(partial, "c").astype(bf16)
    partial = add_over(partial.reshape(Y, ZH * X * 8, 2048), "y").astype(bf16)
    summed = add_over(partial.reshape(ZH, X * 8, 2048), "zh").astype(bf16)
    rows = lax.all_to_all(summed.reshape(X, 8, 2048), "x", split_axis=0, concat_axis=0, tiled=True)
    rows = rows.reshape(X, 8, 16, 128).transpose(1, 2, 0, 3).reshape(8, 8192)

    grad = grad_eigen.reshape(Y * ZH * C, 8, 512)
    grad = lax.all_to_all(grad, ("y", "zh", "c"), split_axis=0, concat_axis=0, tiled=True)
    grad = grad.transpose(1, 0, 2).reshape(8, 8192)
    scaling = rows.astype(f32) / (tokens * Y * ZH * C)
    return (grad.astype(f32) / (scaling + damping)).astype(bf16)


def solution(mesh):
    fine = Mesh(mesh.devices.reshape(Y, ZH, C, 2, 2, 2, 2, X), AXES)
    dp, mp = ("y", "zh", "c"), Z_BITS + ("x",)
    placed = (P(dp, mp), P(dp, mp), P(None, mp), P(None, mp), P(mp, dp))
    return jax.shard_map(
        per_device, mesh=fine, in_specs=placed, out_specs=P(mp + dp, None), check_vma=False
    )
```

```python
import jax
import jax.numpy as jnp
from jax import lax
from jax.sharding import Mesh, PartitionSpec as P

damping = 0.1
Y, ZH, C, X = 4, 2, 2, 4
Z_BITS = ("z8", "z4", "z2", "z1")
AXES = ("y", "zh", "c") + Z_BITS + ("x",)
f32, bf16 = jnp.float32, jnp.bfloat16


def swap(value, axis):
    return lax.ppermute(value, axis, [(0, 1), (1, 0)])


def double_z(have, axis):
    other = swap(have, axis)
    upper = lax.axis_index(axis) == 1
    low = jnp.where(upper, other, have)
    high = jnp.where(upper, have, other)
    return jnp.stack([low, high], axis=1).reshape((-1,) + have.shape[1:])


def basis_over_x(basis):
    blocks = basis.reshape(16, X, 128, 128)
    return lax.all_to_all(blocks, "x", split_axis=1, concat_axis=1, tiled=True)


def add_over(value, axis):
    parts = lax.all_to_all(value, axis, split_axis=0, concat_axis=0, tiled=True)
    return jnp.sum(parts.astype(f32), axis=0)


def together(*values):
    return lax.optimization_barrier(values)


def per_device(activations, out_grads, basis_in, basis_out, grad_eigen):
    tokens = activations.shape[0]
    z_out = double_z(out_grads[None], "z8")
    z_out, z_in = together(z_out, activations[None])
    b_out = basis_over_x(basis_out)
    z_out, z_in = together(double_z(z_out, "z4"), double_z(z_in, "z8"))
    z_out, z_in, b_out, basis_in = together(double_z(z_out, "z2"), double_z(z_in, "z4"), b_out, basis_in)
    b_in = basis_over_x(basis_in)
    z_out, z_in, b_in = together(double_z(z_out, "z1"), double_z(z_in, "z2"), b_in)

    part_out = jnp.einsum("ztf,zxfc->xtc", z_out, b_out, preferred_element_type=f32)
    z_in = double_z(z_in, "z1")
    proj_out = add_over(part_out.astype(bf16), "x")
    squares_out = (proj_out * proj_out).astype(bf16)
    squares_out, z_in = together(squares_out, z_in)

    z_squares = double_z(squares_out[None], "z8")
    part_in = jnp.einsum("zxfc,ztf->xct", b_in, z_in, preferred_element_type=f32)
    proj_in = add_over(part_in.astype(bf16), "x")
    squares_in = (proj_in * proj_in).astype(bf16)
    z_squares, squares_in = together(z_squares, squares_in)

    z_squares = double_z(z_squares, "z4")
    rows_in = lax.all_gather(squares_in, "x", axis=0, tiled=False)
    rows_in = rows_in.reshape(X, Y, ZH, C, 8, tokens)
    rows_in = rows_in.transpose(3, 1, 2, 0, 4, 5).reshape(C * Y * ZH * X * 8, tokens)
    z_squares, rows_in, grad = together(z_squares, rows_in, grad_eigen)

    grad = grad.reshape(Y * ZH * C, 8, 512)
    grad = lax.all_to_all(grad, ("y", "zh", "c"), split_axis=0, concat_axis=0, tiled=True)
    z_squares = double_z(double_z(z_squares, "z2"), "z1")
    z_squares, grad = together(z_squares, grad)
    grad = grad.transpose(1, 0, 2).reshape(8, 8192)

    partial = jnp.einsum("rt,ztc->rzc", rows_in, z_squares, preferred_element_type=f32)
    partial = partial.reshape(C, Y * ZH * X * 8, 2048).astype(bf16)
    partial = add_over(partial, "c").astype(bf16)
    partial = add_over(partial.reshape(Y, ZH * X * 8, 2048), "y").astype(bf16)
    partial = partial.reshape(ZH, X * 8, 2048)
    upper = lax.axis_index("zh") == 1
    other = swap(jnp.where(upper, partial[0], partial[1]), "zh").astype(f32)
    summed = (jnp.where(upper, partial[1], partial[0]).astype(f32) + other).astype(bf16)
    rows = lax.all_to_all(summed.reshape(X, 8, 2048), "x", split_axis=0, concat_axis=0, tiled=True)
    rows = rows.reshape(X, 8, 16, 128).transpose(1, 2, 0, 3).reshape(8, 8192)

    scaling = rows.astype(f32) / (tokens * Y * ZH * C)
    return (grad.astype(f32) / (scaling + damping)).astype(bf16)


def solution(mesh):
    fine = Mesh(mesh.devices.reshape(Y, ZH, C, 2, 2, 2, 2, X), AXES)
    dp, mp = ("y", "zh", "c"), Z_BITS + ("x",)
    placed = (P(dp, mp), P(dp, mp), P(None, mp), P(None, mp), P(mp, dp))
    return jax.shard_map(
        per_device, mesh=fine, in_specs=placed, out_specs=P(mp + dp, None), check_vma=False
    )
```

```python
import jax
import jax.numpy as jnp
from jax import lax
from jax.experimental import pallas as pl
from jax.experimental.pallas import tpu as pltpu
from jax.sharding import Mesh, PartitionSpec as P

damping = 0.1
Y, ZH, C, X = 4, 2, 2, 4
Z_BITS = ("z8", "z4", "z2", "z1")
RING = ("zh",) + Z_BITS
AXES = ("y", "zh", "c") + Z_BITS + ("x",)
f32, bf16 = jnp.float32, jnp.bfloat16
PARAMS = pltpu.CompilerParams(vmem_limit_bytes=16 * 2**20)
SCALAR = pl.BlockSpec(memory_space=pltpu.SMEM)
WHOLE = pl.BlockSpec(memory_space=pltpu.VMEM)
ARRIVAL = [0, 8, 4, 12, 2, 10, 6, 14, 1, 9, 5, 13, 3, 11, 7, 15]


def together(*values):
    return lax.optimization_barrier(values)


def swap(value, axis):
    return lax.ppermute(value, axis, [(0, 1), (1, 0)])


def around(value, hops):
    return lax.ppermute(value, RING, [(i, (i + hops) % 32) for i in range(32)])


def double_z(have, axis):
    return jnp.concatenate([have, swap(have, axis)], axis=0)


def project_kernel(z_ref, near_ref, far_ref, basis_ref, out_ref):
    z = z_ref[0]
    for pair in range(2):
        total = jnp.zeros((256, 256), f32)
        for step in range(8):
            source = near_ref if step < 4 else far_ref
            at = 2 * step if step < 4 else 2 * step - 8
            left = jnp.concatenate([source[at], source[at + 1]], axis=1)
            z0 = z ^ ARRIVAL[2 * step]
            z1 = z ^ ARRIVAL[2 * step + 1]
            columns = [
                jnp.concatenate([basis_ref[2 * pair + i, z0], basis_ref[2 * pair + i, z1]], axis=0) for i in range(2)
            ]
            right = jnp.concatenate(columns, axis=1)
            total = total + jnp.dot(left, right, preferred_element_type=f32)
        out_ref[2 * pair] = total[:, :128].astype(bf16)
        out_ref[2 * pair + 1] = total[:, 128:].astype(bf16)


def project(z, near, far, basis):
    return pl.pallas_call(
        project_kernel,
        out_shape=jax.ShapeDtypeStruct((X, 256, 128), bf16),
        in_specs=[SCALAR, WHOLE, WHOLE, WHOLE],
        out_specs=WHOLE,
        compiler_params=PARAMS,
        cost_estimate=pl.CostEstimate(flops=2 * 256 * 2048 * 512, bytes_accessed=3400000, transcendentals=0),
        name="project",
    )(z, near, far, basis)


def place_kernel(a_ref, *refs):
    *blocks, half_low, half_high, out_ref = refs
    for k, block in zip((0, 1, 2, 3, 5, 6, 7), blocks):
        out_ref[lax.rem(a_ref[0] + k, 8)] = block[...]
    far = lax.rem(a_ref[0] + 4, 8)
    out_ref[far, :128] = half_low[...]
    out_ref[far, 128:] = half_high[...]


def place(a, blocks, halves):
    return pl.pallas_call(
        place_kernel,
        out_shape=jax.ShapeDtypeStruct((8, 256, 128), bf16),
        in_specs=[SCALAR] + [WHOLE] * 9,
        out_specs=WHOLE,
        compiler_params=PARAMS,
        cost_estimate=pl.CostEstimate(flops=0, bytes_accessed=1100000, transcendentals=0),
        name="place",
    )(a, *blocks, *halves)


def scale_kernel(rows_ref, p0, p1, p2a, p2b, p3, out_ref):
    def block(j, at):
        if j == 2:
            return p2a[at] if at < 4 else p2b[at - 4]
        return {0: p0, 1: p1, 3: p3}[j][at]

    for j in range(4):
        for a in (0, 2):
            total = jnp.zeros((256, 256), f32)
            for h in range(2):
                right = jnp.concatenate([block(j, 4 * h + a), block(j, 4 * h + a + 1)], axis=1)
                total = total + jnp.dot(rows_ref[h], right, preferred_element_type=f32)
            total = total.astype(bf16)
            at = (4 * j + a) * 128
            out_ref[0, :, at : at + 256] = total[:128]
            out_ref[1, :, at : at + 256] = total[128:]


def scale_part(rows, p0, p1, p2a, p2b, p3):
    return pl.pallas_call(
        scale_kernel,
        out_shape=jax.ShapeDtypeStruct((C, 128, 2048), bf16),
        in_specs=[WHOLE] * 6,
        out_specs=WHOLE,
        compiler_params=PARAMS,
        cost_estimate=pl.CostEstimate(flops=2 * 256 * 512 * 2048, bytes_accessed=3300000, transcendentals=0),
        name="scale",
    )(rows, p0, p1, p2a, p2b, p3)


def exchange(value, axis):
    return lax.all_to_all(value, axis, split_axis=0, concat_axis=0, tiled=True)


def add_over(value, axis):
    return jnp.sum(exchange(value, axis).astype(f32), axis=0)


def squares(part):
    projected = add_over(part, "x")
    return (projected * projected).astype(bf16)


def per_device(activations, out_grads, basis_in, basis_out, grad_eigen):
    tokens = activations.shape[0]
    ring = lax.axis_index(RING)
    z = (ring % 16).astype(jnp.int32).reshape(1)
    high = lax.axis_index("zh") == 1

    def both(mine):
        kept = jnp.where(high, mine[1], mine[0])
        other = swap(jnp.where(high, mine[0], mine[1]), "zh")
        return jnp.stack([jnp.where(high, other, kept), jnp.where(high, kept, other)])

    basis_out = basis_out.reshape(16, X, 128, 128).transpose(1, 0, 2, 3)
    basis_in = basis_in.reshape(16, X, 128, 128).transpose(1, 0, 2, 3)

    z_out = double_z(out_grads[None], "z8")
    z_out, basis_out = together(z_out, basis_out)
    b_out = exchange(basis_out, "x")
    z_out = double_z(z_out, "z4")
    z_out, z_in = together(z_out, activations[None])
    z_out, z_in, b_out = together(double_z(z_out, "z2"), double_z(z_in, "z8"), b_out)
    z_out, basis_in = together(z_out, basis_in)
    b_in = exchange(basis_in, "x")
    far_out, z_out, z_in = together(swap(z_out, "z1"), z_out, double_z(z_in, "z4"))

    part_out = project(z, z_out, far_out, b_out)
    squares_out = squares(part_out)
    squares_out, z_in, b_in = together(squares_out, double_z(z_in, "z2"), b_in)

    up1, down1, far_in = around(squares_out, 4), around(squares_out, -4), swap(z_in, "z1")
    up1, down1, far_in, z_in = together(up1, down1, far_in, z_in)
    part_in = project(z, z_in, far_in, b_in)
    up2, down2 = around(up1, 4), around(down1, -4)
    squares_in = squares(part_in).T.reshape(Y, ZH, C * 8, tokens).transpose(1, 0, 2, 3)
    up2, down2, squares_in = together(up2, down2, squares_in)
    up3, down3 = around(up2, 4), around(down2, -4)
    rows_in = both(squares_in.reshape(ZH, 64, tokens))
    up3, down3, rows_in = together(up3, down3, rows_in)
    half_low, half_high = around(up3[:128], 4), around(down3[128:], -4)
    half_low, half_high, grad = together(half_low, half_high, grad_eigen)
    p0 = place(
        (ring // 4).astype(jnp.int32).reshape(1), (squares_out, down1, down2, down3, up3, up2, up1), (half_low, half_high)
    )
    p3, p1 = around(p0, 1), around(p0, -1)
    rows_in = lax.all_gather(rows_in, "x", axis=0, tiled=False)
    rows_in = rows_in.reshape(X, ZH, Y, C, 8, tokens).transpose(1, 3, 2, 0, 4, 5).reshape(ZH, 256, tokens)
    grad = both(grad.reshape(Y, ZH, C * 8, 512).transpose(1, 0, 2, 3))
    p3, p1, rows_in, grad = together(p3, p1, rows_in, grad)
    p2a, p2b = around(p1[:4], -1), around(p3[4:], 1)
    grad = grad.reshape(ZH, Y, C, 8, 512).transpose(1, 2, 0, 3, 4).reshape(Y * C, ZH, 8, 512)
    grad = exchange(grad, ("y", "c"))
    p2a, p2b, grad = together(p2a, p2b, grad)
    grad = grad.reshape(Y, C, ZH, 8, 512).transpose(3, 0, 2, 1, 4).reshape(8, 8192)

    partial = scale_part(rows_in, p0, p1, p2a, p2b, p3)
    partial = add_over(partial, "c").astype(bf16)
    summed = add_over(partial.reshape(Y, X * 8, 2048), "y").astype(bf16)
    rows = exchange(summed.reshape(X, 8, 2048), "x").reshape(X, 8, 4, 4, 128)
    rows = rows.transpose(1, 3, 2, 0, 4)
    odd, two = (ring % 2) == 1, ((ring // 2) % 2) == 1
    rows = jnp.where(odd, jnp.roll(rows, 1, axis=2), rows)
    rows = jnp.where(two, jnp.roll(rows, 2, axis=2), rows)
    rows = rows.reshape(8, 8192)

    scaling = rows.astype(f32) / (tokens * Y * ZH * C)
    return (grad.astype(f32) / (scaling + damping)).astype(bf16)


def solution(mesh):
    fine = Mesh(mesh.devices.reshape(Y, ZH, C, 2, 2, 2, 2, X), AXES)
    dp, mp = ("y", "zh", "c"), Z_BITS + ("x",)
    placed = (P(dp, mp), P(dp, mp), P(None, mp), P(None, mp), P(mp, dp))
    return jax.shard_map(
        per_device, mesh=fine, in_specs=placed, out_specs=P(mp + dp, None), check_vma=False
    )
```

```python
import jax
import jax.numpy as jnp
from jax import lax
from jax.experimental import pallas as pl
from jax.experimental.pallas import tpu as pltpu
from jax.sharding import Mesh, PartitionSpec as P

damping = 0.1
Y, ZH, C, X = 4, 2, 2, 4
Z_BITS = ("z8", "z4", "z2", "z1")
RING = ("zh",) + Z_BITS
AXES = ("y", "zh", "c") + Z_BITS + ("x",)
f32, bf16 = jnp.float32, jnp.bfloat16
PARAMS = pltpu.CompilerParams(vmem_limit_bytes=16 * 2**20)
SCALAR = pl.BlockSpec(memory_space=pltpu.SMEM)
WHOLE = pl.BlockSpec(memory_space=pltpu.VMEM)
ARRIVAL = [0, 8, 4, 12, 2, 10, 6, 14, 1, 9, 5, 13, 3, 11, 7, 15]


def together(*values):
    return lax.optimization_barrier(values)


def swap(value, axis):
    return lax.ppermute(value, axis, [(0, 1), (1, 0)])


def around(value, hops):
    return lax.ppermute(value, RING, [(i, (i + hops) % 32) for i in range(32)])


def double_z(have, axis):
    return jnp.concatenate([have, swap(have, axis)], axis=0)


def project_kernel(z_ref, near_ref, far_ref, basis_out_ref, basis_in_ref, out_ref):
    z = z_ref[0]
    for m, basis_ref in enumerate((basis_out_ref, basis_in_ref)):
        for pair in range(2):
            total = jnp.zeros((256, 256), f32)
            for step in range(8):
                source = near_ref if step < 4 else far_ref
                at = 2 * step if step < 4 else 2 * step - 8
                left = jnp.concatenate([source[at, m], source[at + 1, m]], axis=1)
                z0 = z ^ ARRIVAL[2 * step]
                z1 = z ^ ARRIVAL[2 * step + 1]
                columns = [
                    jnp.concatenate([basis_ref[2 * pair + i, z0], basis_ref[2 * pair + i, z1]], axis=0) for i in range(2)
                ]
                right = jnp.concatenate(columns, axis=1)
                total = total + jnp.dot(left, right, preferred_element_type=f32)
            out_ref[2 * pair, m] = total[:, :128].astype(bf16)
            out_ref[2 * pair + 1, m] = total[:, 128:].astype(bf16)


def project(z, near, far, basis_out, basis_in):
    return pl.pallas_call(
        project_kernel,
        out_shape=jax.ShapeDtypeStruct((X, 2, 256, 128), bf16),
        in_specs=[SCALAR] + [WHOLE] * 4,
        out_specs=WHOLE,
        compiler_params=PARAMS,
        cost_estimate=pl.CostEstimate(flops=4 * 256 * 2048 * 512, bytes_accessed=6800000, transcendentals=0),
        name="project",
    )(z, near, far, basis_out, basis_in)


def place_kernel(a_ref, own, *refs):
    *blocks, half_low, half_high, out_ref = refs
    out_ref[a_ref[0]] = own[...]
    for k, block in zip((1, 2, 3, 5, 6, 7), blocks):
        at = lax.rem(a_ref[0] + k, 8)
        out_ref[at, :128] = block[:128]
        out_ref[at, 128:] = block[192:]
    far = lax.rem(a_ref[0] + 4, 8)
    out_ref[far, :128] = half_low[:128]
    out_ref[far, 128:] = half_high[64:]


def place(a, own, blocks, halves):
    return pl.pallas_call(
        place_kernel,
        out_shape=jax.ShapeDtypeStruct((8, 256, 128), bf16),
        in_specs=[SCALAR] + [WHOLE] * 9,
        out_specs=WHOLE,
        compiler_params=PARAMS,
        cost_estimate=pl.CostEstimate(flops=0, bytes_accessed=1100000, transcendentals=0),
        name="place",
    )(a, own, *blocks, *halves)


def scale_kernel(rows_ref, p0, p1, p2a, p2b, p3, out_ref):
    def block(j, at):
        if j == 2:
            return p2a[at] if at < 4 else p2b[at - 4]
        return {0: p0, 1: p1, 3: p3}[j][at]

    for j in range(4):
        for a in (0, 2):
            total = jnp.zeros((256, 256), f32)
            for h in range(2):
                right = jnp.concatenate([block(j, 4 * h + a), block(j, 4 * h + a + 1)], axis=1)
                total = total + jnp.dot(rows_ref[h], right, preferred_element_type=f32)
            at = (4 * j + a) * 128
            out_ref[:, :, at : at + 256] = total.reshape(32, 8, 256).astype(bf16)


def scale_part(rows, p0, p1, p2a, p2b, p3):
    return pl.pallas_call(
        scale_kernel,
        out_shape=jax.ShapeDtypeStruct((X * Y * C, 8, 2048), bf16),
        in_specs=[WHOLE] * 6,
        out_specs=WHOLE,
        compiler_params=PARAMS,
        cost_estimate=pl.CostEstimate(flops=2 * 256 * 512 * 2048, bytes_accessed=3300000, transcendentals=0),
        name="scale",
    )(rows, p0, p1, p2a, p2b, p3)


def exchange(value, axis):
    return lax.all_to_all(value, axis, split_axis=0, concat_axis=0, tiled=True)


def per_device(activations, out_grads, basis_in, basis_out, grad_eigen):
    tokens = activations.shape[0]
    ring = lax.axis_index(RING)
    z = (ring % 16).astype(jnp.int32).reshape(1)
    high = lax.axis_index("zh") == 1

    def mine(halves):
        return jnp.where(high, halves[1], halves[0])

    def theirs(halves):
        return jnp.where(high, halves[0], halves[1])

    def in_order(own, other):
        return jnp.stack([jnp.where(high, other, own), jnp.where(high, own, other)])

    basis_out = basis_out.reshape(16, X, 128, 128).transpose(1, 0, 2, 3)
    basis_in = basis_in.reshape(16, X, 128, 128).transpose(1, 0, 2, 3)

    grad = grad_eigen.reshape(Y, ZH, C * 8, 512).transpose(1, 0, 2, 3)
    grad_own = mine(grad)
    have, grad_other, basis_out = together(
        double_z(jnp.stack([out_grads, activations])[None], "z8"), swap(theirs(grad), "zh"), basis_out
    )
    b_out = exchange(basis_out, "x")
    have, basis_in = together(double_z(have, "z4"), basis_in)
    have, b_out = together(double_z(have, "z2"), b_out)
    b_in = exchange(basis_in, "x")
    far, have, b_in = together(swap(have, "z1"), have, b_in)

    part = project(z, have, far, b_out, b_in)
    projected = jnp.sum(exchange(part, "x").astype(f32), axis=0)
    squares = (projected * projected).astype(bf16)
    squares_out = squares[0]
    squares_in = squares[1].T.reshape(Y, ZH, C * 8, tokens).transpose(1, 0, 2, 3).reshape(ZH, 64, tokens)
    rows_own, rows_sent = mine(squares_in), theirs(squares_in)

    up = jnp.concatenate([squares_out[:128], rows_sent[:, :128], squares_out[128:]], axis=0)
    down = jnp.concatenate([squares_out[:128], rows_sent[:, 128:], squares_out[128:]], axis=0)
    up1, down1 = together(around(up, 4), around(down, -4))
    up2, down2, grad_own, grad_other = together(around(up1, 4), around(down1, -4), grad_own, grad_other)
    grad = in_order(grad_own, grad_other).reshape(ZH, Y, C, 8, 512).transpose(1, 2, 0, 3, 4)
    grad = exchange(grad.reshape(Y * C, ZH, 8, 512), ("y", "c"))
    up3, down3 = together(around(up2, 4), around(down2, -4))
    half_low, half_high, grad = together(around(up3[:192], 4), around(down3[128:], -4), grad)
    p0 = place(
        (ring // 4).astype(jnp.int32).reshape(1),
        squares_out,
        (down1, down2, down3, up3, up2, up1),
        (half_low, half_high),
    )
    rows_other = jnp.concatenate([half_low[128:], half_high[:64]], axis=1)
    rows_in = lax.all_gather(in_order(rows_own, rows_other), "x", axis=0, tiled=False)
    rows_in = rows_in.reshape(X, ZH, Y * C, 8, tokens).transpose(1, 2, 0, 3, 4).reshape(ZH, 256, tokens)
    p3, p1, rows_in = together(around(p0, 1), around(p0, -1), rows_in)
    p2a, p2b = around(p1[:4], -1), around(p3[4:], 1)
    grad = grad.reshape(Y, C, ZH, 8, 512).transpose(3, 0, 2, 1, 4).reshape(8, 8192)
    p2a, p2b, grad = together(p2a, p2b, grad)

    partial = exchange(scale_part(rows_in, p0, p1, p2a, p2b, p3), ("y", "c", "x"))
    rows = jnp.sum(partial.reshape(Y * C, X, 8, 2048).astype(f32), axis=0).reshape(X, 8, 4, 4, 128)
    rows = rows.transpose(1, 3, 2, 0, 4)
    odd, two = (ring % 2) == 1, ((ring // 2) % 2) == 1
    rows = jnp.where(odd, jnp.roll(rows, 1, axis=2), rows)
    rows = jnp.where(two, jnp.roll(rows, 2, axis=2), rows)
    rows = rows.reshape(8, 8192)

    scaling = rows / (tokens * Y * ZH * C)
    return (grad.astype(f32) / (scaling + damping)).astype(bf16)


def solution(mesh):
    fine = Mesh(mesh.devices.reshape(Y, ZH, C, 2, 2, 2, 2, X), AXES)
    dp, mp = ("y", "zh", "c"), Z_BITS + ("x",)
    placed = (P(dp, mp), P(dp, mp), P(None, mp), P(None, mp), P(mp, dp))
    return jax.shard_map(
        per_device, mesh=fine, in_specs=placed, out_specs=P(mp + dp, None), check_vma=False
    )
```

```python
import jax
import jax.numpy as jnp
from jax import lax
from jax.experimental import pallas as pl
from jax.experimental.pallas import tpu as pltpu
from jax.sharding import Mesh, PartitionSpec as P

damping = 0.1
Y, ZH, C, X = 4, 2, 2, 4
Z_BITS = ("z8", "z4", "z2", "z1")
RING = ("zh",) + Z_BITS
AXES = ("y", "zh", "c") + Z_BITS + ("x",)
f32, bf16 = jnp.float32, jnp.bfloat16
PARAMS = pltpu.CompilerParams(vmem_limit_bytes=16 * 2**20)
SCALAR = pl.BlockSpec(memory_space=pltpu.SMEM)
WHOLE = pl.BlockSpec(memory_space=pltpu.VMEM)
ARRIVAL = [0, 8, 4, 12, 2, 10, 6, 14, 1, 9, 5, 13, 3, 11, 7, 15]


def together(*values):
    return lax.optimization_barrier(values)


def swap(value, axis):
    return lax.ppermute(value, axis, [(0, 1), (1, 0)])


def around(value, hops):
    return lax.ppermute(value, RING, [(i, (i + hops) % 32) for i in range(32)])


def double_z(have, axis):
    return jnp.concatenate([have, swap(have, axis)], axis=0)


def project_kernel(z_ref, near_ref, far_ref, basis_ref, out_ref):
    z = z_ref[0]
    for pair in range(2):
        total = jnp.zeros((256, 256), f32)
        for step in range(8):
            source = near_ref if step < 4 else far_ref
            at = 2 * step if step < 4 else 2 * step - 8
            left = jnp.concatenate([source[at], source[at + 1]], axis=1)
            z0 = z ^ ARRIVAL[2 * step]
            z1 = z ^ ARRIVAL[2 * step + 1]
            columns = [
                jnp.concatenate([basis_ref[2 * pair + i, z0], basis_ref[2 * pair + i, z1]], axis=0) for i in range(2)
            ]
            right = jnp.concatenate(columns, axis=1)
            total = total + jnp.dot(left, right, preferred_element_type=f32)
        out_ref[2 * pair] = total[:, :128].astype(bf16)
        out_ref[2 * pair + 1] = total[:, 128:].astype(bf16)


def project(z, near, far, basis):
    return pl.pallas_call(
        project_kernel,
        out_shape=jax.ShapeDtypeStruct((X, 256, 128), bf16),
        in_specs=[SCALAR] + [WHOLE] * 3,
        out_specs=WHOLE,
        compiler_params=PARAMS,
        cost_estimate=pl.CostEstimate(flops=20 * 2**30, bytes_accessed=3400000, transcendentals=0),
        name="project",
    )(z, near, far, basis)


def place_kernel(a_ref, own, *refs):
    *blocks, half_low, half_high, out_ref = refs
    out_ref[a_ref[0]] = own[...]
    for k, block in zip((1, 2, 3, 5, 6, 7), blocks):
        at = lax.rem(a_ref[0] + k, 8)
        out_ref[at, :128] = block[:128]
        out_ref[at, 128:] = block[128:]
    far = lax.rem(a_ref[0] + 4, 8)
    out_ref[far, :128] = half_low[...]
    out_ref[far, 128:] = half_high[...]


def place(a, own, blocks, halves):
    return pl.pallas_call(
        place_kernel,
        out_shape=jax.ShapeDtypeStruct((8, 256, 128), bf16),
        in_specs=[SCALAR] + [WHOLE] * 9,
        out_specs=WHOLE,
        compiler_params=PARAMS,
        cost_estimate=pl.CostEstimate(flops=0, bytes_accessed=1100000, transcendentals=0),
        name="place",
    )(a, own, *blocks, *halves)


def scale_kernel(rows_ref, p0, p1, p2a, p2b, p3, out_ref):
    def block(j, at):
        if j == 2:
            return p2a[at] if at < 4 else p2b[at - 4]
        return {0: p0, 1: p1, 3: p3}[j][at]

    for j in range(4):
        for a in (0, 2):
            total = jnp.zeros((256, 256), f32)
            for h in range(2):
                right = jnp.concatenate([block(j, 4 * h + a), block(j, 4 * h + a + 1)], axis=1)
                total = total + jnp.dot(rows_ref[h], right, preferred_element_type=f32)
            at = (4 * j + a) * 128
            out_ref[:, :, at : at + 256] = total.reshape(32, 8, 256).astype(bf16)


def scale_part(rows, p0, p1, p2a, p2b, p3):
    return pl.pallas_call(
        scale_kernel,
        out_shape=jax.ShapeDtypeStruct((X * Y * C, 8, 2048), bf16),
        in_specs=[WHOLE] * 6,
        out_specs=WHOLE,
        compiler_params=PARAMS,
        cost_estimate=pl.CostEstimate(flops=2 * 256 * 512 * 2048, bytes_accessed=3300000, transcendentals=0),
        name="scale",
    )(rows, p0, p1, p2a, p2b, p3)


def exchange(value, axis):
    return lax.all_to_all(value, axis, split_axis=0, concat_axis=0, tiled=True)


def per_device(activations, out_grads, basis_in, basis_out, grad_eigen):
    tokens = activations.shape[0]
    ring = lax.axis_index(RING)
    z = (ring % 16).astype(jnp.int32).reshape(1)
    high = lax.axis_index("zh") == 1

    def mine(halves):
        return jnp.where(high, halves[1], halves[0])

    def theirs(halves):
        return jnp.where(high, halves[0], halves[1])

    def in_order(own, other):
        return jnp.stack([jnp.where(high, other, own), jnp.where(high, own, other)])

    def squares(part):
        projected = jnp.sum(part.astype(f32), axis=0)
        return (projected * projected).astype(bf16)

    basis_out = basis_out.reshape(16, X, 128, 128).transpose(1, 0, 2, 3)
    basis_in = basis_in.reshape(16, X, 128, 128).transpose(1, 0, 2, 3)

    b_in = exchange(basis_in, "x")
    z_in, z_out, grad_eigen = together(double_z(activations[None], "z8"), out_grads[None], grad_eigen)
    z_in, z_out, b_in, basis_out = together(double_z(z_in, "z4"), double_z(z_out, "z8"), b_in, basis_out)
    grad = grad_eigen.reshape(Y, ZH, C, 8, 512).transpose(0, 2, 1, 3, 4).reshape(Y * C, ZH, 8, 512)
    grad = exchange(grad, ("y", "c"))
    z_in, z_out, grad, basis_out = together(double_z(z_in, "z2"), double_z(z_out, "z4"), grad, basis_out)
    b_out = exchange(basis_out, "x")
    far_in, z_in, z_out, b_out = together(swap(z_in, "z1"), z_in, double_z(z_out, "z2"), b_out)

    far_out = swap(z_out, "z1")
    squares_in = squares(exchange(project(z, z_in, far_in, b_in), "x"))
    squares_in = squares_in.T.reshape(Y, ZH, C * 8, tokens).transpose(1, 0, 2, 3).reshape(ZH, 64, tokens)
    far_out, z_out, b_out, squares_in, grad = together(far_out, z_out, b_out, squares_in, grad)
    grad = grad.transpose(1, 0, 2, 3)

    sent = jnp.concatenate([theirs(squares_in), theirs(grad).reshape(64, 512)], axis=1)
    got = swap(sent, "zh")
    part_out, got = together(exchange(project(z, z_out, far_out, b_out), "x"), got)
    squares_out = squares(part_out)
    rows_in = in_order(mine(squares_in), got[:, :tokens])
    grad = in_order(mine(grad), got[:, tokens:].reshape(Y * C, 8, 512))
    grad = grad.reshape(ZH, Y, C, 8, 512).transpose(3, 1, 0, 2, 4).reshape(8, 8192)

    up1, down1 = together(around(squares_out, 4), around(squares_out, -4))
    up2, down2 = together(around(up1, 4), around(down1, -4))
    up3, down3 = together(around(up2, 4), around(down2, -4))
    half_low, half_high, grad, rows_in = together(around(up3[:128], 4), around(down3[128:], -4), grad, rows_in)
    p0 = place(
        (ring // 4).astype(jnp.int32).reshape(1),
        squares_out,
        (down1, down2, down3, up3, up2, up1),
        (half_low, half_high),
    )
    rows_in = lax.all_gather(rows_in, "x", axis=0, tiled=False)
    rows_in = rows_in.reshape(X, ZH, Y * C, 8, tokens).transpose(1, 2, 0, 3, 4).reshape(ZH, 256, tokens)
    p3, p1, rows_in = together(around(p0, 1), around(p0, -1), rows_in)
    p2a, p2b = around(p1[:4], -1), around(p3[4:], 1)

    partial = exchange(scale_part(rows_in, p0, p1, p2a, p2b, p3), ("y", "c", "x"))
    rows = jnp.sum(partial.reshape(Y * C, X, 8, 2048).astype(f32), axis=0).reshape(X, 8, 4, 4, 128)
    rows = rows.transpose(1, 3, 2, 0, 4)
    odd, two = (ring % 2) == 1, ((ring // 2) % 2) == 1
    rows = jnp.where(odd, jnp.roll(rows, 1, axis=2), rows)
    rows = jnp.where(two, jnp.roll(rows, 2, axis=2), rows)
    rows = rows.reshape(8, 8192)

    scaling = rows / (tokens * Y * ZH * C)
    return (grad.astype(f32) / (scaling + damping)).astype(bf16)


def solution(mesh):
    fine = Mesh(mesh.devices.reshape(Y, ZH, C, 2, 2, 2, 2, X), AXES)
    dp, mp = ("y", "zh", "c"), Z_BITS + ("x",)
    placed = (P(dp, mp), P(dp, mp), P(None, mp), P(None, mp), P(mp, dp))
    return jax.shard_map(
        per_device, mesh=fine, in_specs=placed, out_specs=P(mp + dp, None), check_vma=False
    )
```

```python
import jax
import jax.numpy as jnp
from jax import lax
from jax.experimental import pallas as pl
from jax.experimental.pallas import tpu as pltpu
from jax.sharding import Mesh, PartitionSpec as P

damping = 0.1
Y, ZH, C, X = 4, 2, 2, 4
Z_BITS = ("z8", "z4", "z2", "z1")
RING = ("zh",) + Z_BITS
AXES = ("y", "zh", "c") + Z_BITS + ("x",)
f32, bf16 = jnp.float32, jnp.bfloat16
PARAMS = pltpu.CompilerParams(vmem_limit_bytes=16 * 2**20)
SCALAR = pl.BlockSpec(memory_space=pltpu.SMEM)
WHOLE = pl.BlockSpec(memory_space=pltpu.VMEM)
def together(*values):
    return lax.optimization_barrier(values)


def swap(value, axis):
    return lax.ppermute(value, axis, [(0, 1), (1, 0)])


def around(value, hops):
    return lax.ppermute(value, RING, [(i, (i + hops) % 32) for i in range(32)])


def project_kernel(z_ref, near_ref, far_ref, basis_out_ref, basis_in_ref, out_ref):
    residue = lax.rem(z_ref[0], 4)
    for m, basis_ref in enumerate((basis_out_ref, basis_in_ref)):
        for pair in range(2):
            total = jnp.zeros((256, 256), f32)
            for step in range(8):
                source = near_ref if step < 4 else far_ref
                at = 2 * (step % 4)
                left = jnp.concatenate([source[at, m], source[at + 1, m]], axis=1)
                z0 = 4 * (at % 4) + (residue ^ (2 * (at // 4) + step // 4))
                z1 = z0 + 4
                columns = [
                    jnp.concatenate([basis_ref[2 * pair + i, z0], basis_ref[2 * pair + i, z1]], axis=0) for i in range(2)
                ]
                right = jnp.concatenate(columns, axis=1)
                total = total + jnp.dot(left, right, preferred_element_type=f32)
            out_ref[2 * pair, m] = total[:, :128].astype(bf16)
            out_ref[2 * pair + 1, m] = total[:, 128:].astype(bf16)


def project(z, near, far, basis_out, basis_in):
    return pl.pallas_call(
        project_kernel,
        out_shape=jax.ShapeDtypeStruct((X, 2, 256, 128), bf16),
        in_specs=[SCALAR] + [WHOLE] * 4,
        out_specs=WHOLE,
        compiler_params=PARAMS,
        cost_estimate=pl.CostEstimate(flops=4 * 256 * 2048 * 512, bytes_accessed=6800000, transcendentals=0),
        name="project",
    )(z, near, far, basis_out, basis_in)


def scale_kernel(rows_ref, p0, p1, p2a, p2b, p3, out_ref):
    def block(j, at):
        if j == 2:
            return p2a[at] if at < 4 else p2b[at - 4]
        return {0: p0, 1: p1, 3: p3}[j][at]

    for j in range(4):
        for a in (0, 2):
            total = jnp.zeros((256, 256), f32)
            for h in range(2):
                right = jnp.concatenate([block(j, 4 * h + a), block(j, 4 * h + a + 1)], axis=1)
                total = total + jnp.dot(rows_ref[h], right, preferred_element_type=f32)
            at = (4 * j + a) * 128
            out_ref[:, :, at : at + 256] = total.reshape(32, 8, 256).astype(bf16)


def scale_part(rows, p0, p1, p2a, p2b, p3):
    return pl.pallas_call(
        scale_kernel,
        out_shape=jax.ShapeDtypeStruct((X * Y * C, 8, 2048), bf16),
        in_specs=[WHOLE] * 6,
        out_specs=WHOLE,
        compiler_params=PARAMS,
        cost_estimate=pl.CostEstimate(flops=2 * 256 * 512 * 2048, bytes_accessed=3300000, transcendentals=0),
        name="scale",
    )(rows, p0, p1, p2a, p2b, p3)


def exchange(value, axis):
    return lax.all_to_all(value, axis, split_axis=0, concat_axis=0, tiled=True)


def per_device(activations, out_grads, basis_in, basis_out, grad_eigen):
    tokens = activations.shape[0]
    ring = lax.axis_index(RING)
    z = (ring % 16).astype(jnp.int32).reshape(1)
    high = lax.axis_index("zh") == 1

    def mine(halves):
        return jnp.where(high, halves[1], halves[0])

    def theirs(halves):
        return jnp.where(high, halves[0], halves[1])

    def in_order(own, other):
        return jnp.stack([jnp.where(high, other, own), jnp.where(high, own, other)])

    basis_out = basis_out.reshape(16, X, 128, 128).transpose(1, 0, 2, 3)

    b_out = exchange(basis_out, "x")
    have = lax.all_gather(jnp.stack([out_grads, activations]), ("z8", "z4"), axis=0, tiled=False)
    have, b_out, basis_in, grad_eigen = together(have, b_out, basis_in, grad_eigen)
    b_in = exchange(basis_in.reshape(16, X, 128, 128).transpose(1, 0, 2, 3), "x")
    have = jnp.concatenate([have, swap(have, "z2")], axis=0)
    have, b_in, grad_eigen = together(have, b_in, grad_eigen)
    grad = grad_eigen.reshape(Y, ZH, C, 8, 512).transpose(0, 2, 1, 3, 4).reshape(Y * C, ZH, 8, 512)
    grad = exchange(grad, ("y", "c"))
    far, have, grad = together(swap(have, "z1"), have, grad)
    grad = grad.transpose(1, 0, 2, 3)

    part = project(z, have, far, b_out, b_in)
    projected = jnp.sum(exchange(part, "x").astype(f32), axis=0)
    squares = (projected * projected).astype(bf16)
    squares_in = squares[1].T.reshape(Y, ZH, C * 8, tokens).transpose(1, 0, 2, 3).reshape(ZH, 64, tokens)

    sent = jnp.concatenate([theirs(squares_in), theirs(grad).reshape(64, 512)], axis=1)
    p0 = lax.all_gather(squares[0], ("zh", "z8", "z4"), axis=0, tiled=False)
    p0, got = together(p0, swap(sent, "zh"))
    rows_in = in_order(mine(squares_in), got[:, :tokens])
    rows_in = lax.all_gather(rows_in, "x", axis=0, tiled=False)
    rows_in = rows_in.reshape(X, ZH, Y * C, 8, tokens).transpose(1, 2, 0, 3, 4).reshape(ZH, 256, tokens)
    grad = in_order(mine(grad), got[:, tokens:].reshape(Y * C, 8, 512))
    grad = grad.reshape(ZH, Y, C, 8, 512).transpose(3, 1, 0, 2, 4).reshape(8, 8192)
    p3, p1, rows_in = together(around(p0, 1), around(p0, -1), rows_in)
    p2a, p2b, grad = together(around(p1[:4], -1), around(p3[4:], 1), grad)

    partial = exchange(scale_part(rows_in, p0, p1, p2a, p2b, p3), ("y", "c", "x"))
    rows = jnp.sum(partial.reshape(Y * C, X, 8, 2048).astype(f32), axis=0).reshape(X, 8, 4, 4, 128)
    rows = rows.transpose(1, 3, 2, 0, 4)
    odd, two = (ring % 2) == 1, ((ring // 2) % 2) == 1
    rows = jnp.where(odd, jnp.roll(rows, 1, axis=2), rows)
    rows = jnp.where(two, jnp.roll(rows, 2, axis=2), rows)
    rows = rows.reshape(8, 8192)

    scaling = rows / (tokens * Y * ZH * C)
    return (grad.astype(f32) / (scaling + damping)).astype(bf16)


def solution(mesh):
    fine = Mesh(mesh.devices.reshape(Y, ZH, C, 2, 2, 2, 2, X), AXES)
    dp, mp = ("y", "zh", "c"), Z_BITS + ("x",)
    placed = (P(dp, mp), P(dp, mp), P(None, mp), P(None, mp), P(mp, dp))
    return jax.shard_map(
        per_device, mesh=fine, in_specs=placed, out_specs=P(mp + dp, None), check_vma=False
    )
```

```python
import jax
import jax.numpy as jnp
from jax import lax
from jax.experimental import pallas as pl
from jax.experimental.pallas import tpu as pltpu
from jax.sharding import Mesh, PartitionSpec as P

damping = 0.1
Y, ZH, C, X = 4, 2, 2, 4
Z_BITS = ("z8", "z4", "z2", "z1")
RING = ("zh",) + Z_BITS
AXES = ("y", "zh", "c") + Z_BITS + ("x",)
f32, bf16 = jnp.float32, jnp.bfloat16
PARAMS = pltpu.CompilerParams(vmem_limit_bytes=16 * 2**20)
SCALAR = pl.BlockSpec(memory_space=pltpu.SMEM)
WHOLE = pl.BlockSpec(memory_space=pltpu.VMEM)
def together(*values):
    return lax.optimization_barrier(values)


def swap(value, axis):
    return lax.ppermute(value, axis, [(0, 1), (1, 0)])


def around(value, hops):
    return lax.ppermute(value, RING, [(i, (i + hops) % 32) for i in range(32)])


def project_kernel(z_ref, near_ref, far_ref, basis_out_ref, basis_in_ref, out_ref):
    residue = lax.rem(z_ref[0], 4)
    for m, basis_ref in enumerate((basis_out_ref, basis_in_ref)):
        for pair in range(2):
            total = jnp.zeros((256, 256), f32)
            for step in range(8):
                source = near_ref if step < 4 else far_ref
                at = 2 * (step % 4)
                left = jnp.concatenate([source[at, m], source[at + 1, m]], axis=1)
                z0 = 4 * (at % 4) + (residue ^ (2 * (at // 4) + step // 4))
                z1 = z0 + 4
                columns = [
                    jnp.concatenate([basis_ref[2 * pair + i, z0], basis_ref[2 * pair + i, z1]], axis=0) for i in range(2)
                ]
                right = jnp.concatenate(columns, axis=1)
                total = total + jnp.dot(left, right, preferred_element_type=f32)
            out_ref[2 * pair, m] = total[:, :128].astype(bf16)
            out_ref[2 * pair + 1, m] = total[:, 128:].astype(bf16)


def project(z, near, far, basis_out, basis_in):
    return pl.pallas_call(
        project_kernel,
        out_shape=jax.ShapeDtypeStruct((X, 2, 256, 128), bf16),
        in_specs=[SCALAR] + [WHOLE] * 4,
        out_specs=WHOLE,
        compiler_params=PARAMS,
        cost_estimate=pl.CostEstimate(flops=4 * 256 * 2048 * 512, bytes_accessed=6800000, transcendentals=0),
        name="project",
    )(z, near, far, basis_out, basis_in)


def place_kernel(a_ref, own, *refs):
    *blocks, half_low, half_high, out_ref = refs
    out_ref[a_ref[0]] = own[...]
    for k, block in zip((1, 2, 3, 5, 6, 7), blocks):
        at = lax.rem(a_ref[0] + k, 8)
        out_ref[at, :128] = block[:128]
        out_ref[at, 128:] = block[192:]
    far = lax.rem(a_ref[0] + 4, 8)
    out_ref[far, :128] = half_low[:128]
    out_ref[far, 128:] = half_high[64:]


def place(a, own, blocks, halves):
    return pl.pallas_call(
        place_kernel,
        out_shape=jax.ShapeDtypeStruct((8, 256, 128), bf16),
        in_specs=[SCALAR] + [WHOLE] * 9,
        out_specs=WHOLE,
        compiler_params=PARAMS,
        cost_estimate=pl.CostEstimate(flops=0, bytes_accessed=1100000, transcendentals=0),
        name="place",
    )(a, own, *blocks, *halves)


def scale_kernel(rows_ref, p0, p1, p2a, p2b, p3, out_ref):
    def block(j, at):
        if j == 2:
            return p2a[at] if at < 4 else p2b[at - 4]
        return {0: p0, 1: p1, 3: p3}[j][at]

    for j in range(4):
        for a in (0, 2):
            total = jnp.zeros((256, 256), f32)
            for h in range(2):
                right = jnp.concatenate([block(j, 4 * h + a), block(j, 4 * h + a + 1)], axis=1)
                total = total + jnp.dot(rows_ref[h], right, preferred_element_type=f32)
            at = (4 * j + a) * 128
            out_ref[:, :, at : at + 256] = total.reshape(32, 8, 256).astype(bf16)


def scale_part(rows, p0, p1, p2a, p2b, p3):
    return pl.pallas_call(
        scale_kernel,
        out_shape=jax.ShapeDtypeStruct((X * Y * C, 8, 2048), bf16),
        in_specs=[WHOLE] * 6,
        out_specs=WHOLE,
        compiler_params=PARAMS,
        cost_estimate=pl.CostEstimate(flops=2 * 256 * 512 * 2048, bytes_accessed=3300000, transcendentals=0),
        name="scale",
    )(rows, p0, p1, p2a, p2b, p3)


def exchange(value, axis):
    return lax.all_to_all(value, axis, split_axis=0, concat_axis=0, tiled=True)


def per_device(activations, out_grads, basis_in, basis_out, grad_eigen):
    tokens = activations.shape[0]
    ring = lax.axis_index(RING)
    z = (ring % 16).astype(jnp.int32).reshape(1)
    high = lax.axis_index("zh") == 1

    def mine(halves):
        return jnp.where(high, halves[1], halves[0])

    def theirs(halves):
        return jnp.where(high, halves[0], halves[1])

    def in_order(own, other):
        return jnp.stack([jnp.where(high, other, own), jnp.where(high, own, other)])

    basis_out = basis_out.reshape(16, X, 128, 128).transpose(1, 0, 2, 3)

    basis_in = basis_in.reshape(16, X, 128, 128).transpose(1, 0, 2, 3)

    grad = grad_eigen.reshape(Y, ZH, C, 8, 512).transpose(0, 2, 1, 3, 4).reshape(Y * C, ZH, 8, 512)
    grad = exchange(grad, ("y", "c"))
    have, basis_out = together(jnp.stack([out_grads, activations]), basis_out)
    have = lax.all_gather(have, ("z8", "z4"), axis=0, tiled=False)
    have, grad, basis_out = together(have, grad, basis_out)
    b_out = exchange(basis_out, "x")
    have = jnp.concatenate([have, swap(have, "z2")], axis=0)
    have, b_out, basis_in = together(have, b_out, basis_in)
    b_in = exchange(basis_in, "x")
    grad = grad.transpose(1, 0, 2, 3)
    grad_own, grad_other = mine(grad), swap(theirs(grad), "zh")
    far, have, b_in, grad_own, grad_other = together(swap(have, "z1"), have, b_in, grad_own, grad_other)

    part = project(z, have, far, b_out, b_in)
    projected = jnp.sum(exchange(part, "x").astype(f32), axis=0)
    squares = (projected * projected).astype(bf16)
    squares_out = squares[0]
    squares_in = squares[1].T.reshape(Y, ZH, C * 8, tokens).transpose(1, 0, 2, 3).reshape(ZH, 64, tokens)
    rows_own, rows_sent = mine(squares_in), theirs(squares_in)

    up = jnp.concatenate([squares_out[:128], rows_sent[:, :128], squares_out[128:]], axis=0)
    down = jnp.concatenate([squares_out[:128], rows_sent[:, 128:], squares_out[128:]], axis=0)
    up1, down1 = together(around(up, 4), around(down, -4))
    grad = in_order(grad_own, grad_other)
    grad = grad.reshape(ZH, Y, C, 8, 512).transpose(3, 1, 0, 2, 4).reshape(8, 8192)
    up2, down2, grad = together(around(up1, 4), around(down1, -4), grad)
    up3, down3 = together(around(up2, 4), around(down2, -4))
    half_low, half_high = together(around(up3[:192], 4), around(down3[128:], -4))
    p0 = place(
        (ring // 4).astype(jnp.int32).reshape(1),
        squares_out,
        (down1, down2, down3, up3, up2, up1),
        (half_low, half_high),
    )
    rows_other = jnp.concatenate([half_low[128:], half_high[:64]], axis=1)
    rows_in = lax.all_gather(in_order(rows_own, rows_other), "x", axis=0, tiled=False)
    rows_in = rows_in.reshape(X, ZH, Y * C, 8, tokens).transpose(1, 2, 0, 3, 4).reshape(ZH, 256, tokens)
    p3, p1, rows_in = together(around(p0, 1), around(p0, -1), rows_in)
    p2a, p2b, grad = together(around(p1[:4], -1), around(p3[4:], 1), grad)

    partial = exchange(scale_part(rows_in, p0, p1, p2a, p2b, p3), ("y", "c", "x"))
    rows = jnp.sum(partial.reshape(Y * C, X, 8, 2048).astype(f32), axis=0).reshape(X, 8, 4, 4, 128)
    rows = rows.transpose(1, 3, 2, 0, 4)
    odd, two = (ring % 2) == 1, ((ring // 2) % 2) == 1
    rows = jnp.where(odd, jnp.roll(rows, 1, axis=2), rows)
    rows = jnp.where(two, jnp.roll(rows, 2, axis=2), rows)
    rows = rows.reshape(8, 8192)

    scaling = rows / (tokens * Y * ZH * C)
    return (grad.astype(f32) / (scaling + damping)).astype(bf16)


def solution(mesh):
    fine = Mesh(mesh.devices.reshape(Y, ZH, C, 2, 2, 2, 2, X), AXES)
    dp, mp = ("y", "zh", "c"), Z_BITS + ("x",)
    placed = (P(dp, mp), P(dp, mp), P(None, mp), P(None, mp), P(mp, dp))
    return jax.shard_map(
        per_device, mesh=fine, in_specs=placed, out_specs=P(mp + dp, None), check_vma=False
    )
```

```python
import jax
import jax.numpy as jnp
from jax import lax
from jax.experimental import pallas as pl
from jax.experimental.pallas import tpu as pltpu
from jax.sharding import Mesh, PartitionSpec as P

damping = 0.1
Y, ZH, C, X = 4, 2, 2, 4
Z_BITS = ("z8", "z4", "z2", "z1")
RING = ("zh",) + Z_BITS
AXES = ("y", "zh", "c") + Z_BITS + ("x",)
f32, bf16 = jnp.float32, jnp.bfloat16
PARAMS = pltpu.CompilerParams(vmem_limit_bytes=16 * 2**20)
SCALAR = pl.BlockSpec(memory_space=pltpu.SMEM)
WHOLE = pl.BlockSpec(memory_space=pltpu.VMEM)
def together(*values):
    return lax.optimization_barrier(values)


def swap(value, axis):
    return lax.ppermute(value, axis, [(0, 1), (1, 0)])


def around(value, hops):
    return lax.ppermute(value, RING, [(i, (i + hops) % 32) for i in range(32)])


def project_kernel(z_ref, near_ref, far_ref, basis_ref, out_ref):
    residue = lax.rem(z_ref[0], 4)
    for m in range(2):
        for pair in range(2):
            total = jnp.zeros((256, 256), f32)
            for step in range(8):
                source = near_ref if step < 4 else far_ref
                at = 2 * (step % 4)
                left = jnp.concatenate([source[at, m], source[at + 1, m]], axis=1)
                z0 = 4 * (at % 4) + (residue ^ (2 * (at // 4) + step // 4))
                z1 = z0 + 4
                columns = [
                    jnp.concatenate([basis_ref[2 * pair + i, m, z0], basis_ref[2 * pair + i, m, z1]], axis=0) for i in range(2)
                ]
                right = jnp.concatenate(columns, axis=1)
                total = total + jnp.dot(left, right, preferred_element_type=f32)
            out_ref[2 * pair, m] = total[:, :128].astype(bf16)
            out_ref[2 * pair + 1, m] = total[:, 128:].astype(bf16)


def project(z, near, far, basis):
    return pl.pallas_call(
        project_kernel,
        out_shape=jax.ShapeDtypeStruct((X, 2, 256, 128), bf16),
        in_specs=[SCALAR] + [WHOLE] * 3,
        out_specs=WHOLE,
        compiler_params=PARAMS,
        cost_estimate=pl.CostEstimate(flops=4 * 256 * 2048 * 512, bytes_accessed=6800000, transcendentals=0),
        name="project",
    )(z, near, far, basis)


def scale_kernel(rows_ref, p0, p1, p2a, p2b, p3, out_ref):
    def block(j, at):
        if j == 2:
            return p2a[at] if at < 4 else p2b[at - 4]
        return {0: p0, 1: p1, 3: p3}[j][at]

    for j in range(4):
        for a in (0, 2):
            total = jnp.zeros((256, 256), f32)
            for h in range(2):
                right = jnp.concatenate([block(j, 4 * h + a), block(j, 4 * h + a + 1)], axis=1)
                total = total + jnp.dot(rows_ref[h], right, preferred_element_type=f32)
            at = (4 * j + a) * 128
            out_ref[:, :, at : at + 256] = total.reshape(32, 8, 256).astype(bf16)


def scale_part(rows, p0, p1, p2a, p2b, p3):
    return pl.pallas_call(
        scale_kernel,
        out_shape=jax.ShapeDtypeStruct((X * Y * C, 8, 2048), bf16),
        in_specs=[WHOLE] * 6,
        out_specs=WHOLE,
        compiler_params=PARAMS,
        cost_estimate=pl.CostEstimate(flops=2 * 256 * 512 * 2048, bytes_accessed=3300000, transcendentals=0),
        name="scale",
    )(rows, p0, p1, p2a, p2b, p3)


def exchange(value, axis):
    return lax.all_to_all(value, axis, split_axis=0, concat_axis=0, tiled=True)


def per_device(activations, out_grads, basis_in, basis_out, grad_eigen):
    tokens = activations.shape[0]
    ring = lax.axis_index(RING)
    z = (ring % 16).astype(jnp.int32).reshape(1)
    high = lax.axis_index("zh") == 1

    def mine(halves):
        return jnp.where(high, halves[1], halves[0])

    def theirs(halves):
        return jnp.where(high, halves[0], halves[1])

    def in_order(own, other):
        return jnp.stack([jnp.where(high, other, own), jnp.where(high, own, other)])

    bases = jnp.stack([basis_out.reshape(16, X, 128, 128), basis_in.reshape(16, X, 128, 128)])
    bases = exchange(bases.transpose(2, 0, 1, 3, 4), "x")

    have = lax.all_gather(jnp.stack([out_grads, activations]), ("z8", "z4"), axis=0, tiled=False)
    have = jnp.concatenate([have, swap(have, "z2")], axis=0)
    have, bases, grad_eigen = together(have, bases, grad_eigen)
    grad = grad_eigen.reshape(Y, ZH, C, 8, 512).transpose(0, 2, 1, 3, 4).reshape(Y * C, ZH, 8, 512)
    grad = exchange(grad, ("y", "c"))
    far, have, grad = together(swap(have, "z1"), have, grad)
    grad = grad.transpose(1, 0, 2, 3)

    part = project(z, have, far, bases)
    projected = jnp.sum(exchange(part, "x").astype(f32), axis=0)
    squares = (projected * projected).astype(bf16)
    squares_in = squares[1].T.reshape(Y, ZH, C * 8, tokens).transpose(1, 0, 2, 3).reshape(ZH, 64, tokens)

    sent = jnp.concatenate([theirs(squares_in), theirs(grad).reshape(64, 512)], axis=1)
    p0 = lax.all_gather(squares[0], ("zh", "z8", "z4"), axis=0, tiled=False)
    p0, got = together(p0, swap(sent, "zh"))
    rows_in = in_order(mine(squares_in), got[:, :tokens])
    rows_in = lax.all_gather(rows_in, "x", axis=0, tiled=False)
    rows_in = rows_in.reshape(X, ZH, Y * C, 8, tokens).transpose(1, 2, 0, 3, 4).reshape(ZH, 256, tokens)
    grad = in_order(mine(grad), got[:, tokens:].reshape(Y * C, 8, 512))
    grad = grad.reshape(ZH, Y, C, 8, 512).transpose(3, 1, 0, 2, 4).reshape(8, 8192)
    p3, p1, rows_in = together(around(p0, 1), around(p0, -1), rows_in)
    p2a, p2b, grad = together(around(p1[:4], -1), around(p3[4:], 1), grad)

    partial = exchange(scale_part(rows_in, p0, p1, p2a, p2b, p3), ("y", "c", "x"))
    rows = jnp.sum(partial.reshape(Y * C, X, 8, 2048).astype(f32), axis=0).reshape(X, 8, 4, 4, 128)
    rows = rows.transpose(1, 3, 2, 0, 4)
    odd, two = (ring % 2) == 1, ((ring // 2) % 2) == 1
    rows = jnp.where(odd, jnp.roll(rows, 1, axis=2), rows)
    rows = jnp.where(two, jnp.roll(rows, 2, axis=2), rows)
    rows = rows.reshape(8, 8192)

    scaling = rows / (tokens * Y * ZH * C)
    return (grad.astype(f32) / (scaling + damping)).astype(bf16)


def solution(mesh):
    fine = Mesh(mesh.devices.reshape(Y, ZH, C, 2, 2, 2, 2, X), AXES)
    dp, mp = ("y", "zh", "c"), Z_BITS + ("x",)
    placed = (P(dp, mp), P(dp, mp), P(None, mp), P(None, mp), P(mp, dp))
    return jax.shard_map(
        per_device, mesh=fine, in_specs=placed, out_specs=P(mp + dp, None), check_vma=False
    )
```

```python
import jax
import jax.numpy as jnp
from jax import lax
from jax.experimental import pallas as pl
from jax.experimental.pallas import tpu as pltpu
from jax.sharding import Mesh, PartitionSpec as P

damping = 0.1
Y, ZH, C, X = 4, 2, 2, 4
Z_BITS = ("z8", "z4", "z2", "z1")
RING = ("zh",) + Z_BITS
AXES = ("y", "zh", "c") + Z_BITS + ("x",)
f32, bf16 = jnp.float32, jnp.bfloat16
PARAMS = pltpu.CompilerParams(vmem_limit_bytes=16 * 2**20)
SCALAR = pl.BlockSpec(memory_space=pltpu.SMEM)
WHOLE = pl.BlockSpec(memory_space=pltpu.VMEM)
def together(*values):
    return lax.optimization_barrier(values)


def swap(value, axis):
    return lax.ppermute(value, axis, [(0, 1), (1, 0)])


def around(value, hops):
    return lax.ppermute(value, RING, [(i, (i + hops) % 32) for i in range(32)])


def project_kernel(z_ref, near_ref, far_ref, basis_ref, out_ref):
    residue = lax.rem(z_ref[0], 4)
    for m in range(2):
        for pair in range(2):
            total = jnp.zeros((256, 256), f32)
            for step in range(8):
                source = near_ref if step < 4 else far_ref
                at = 2 * (step % 4)
                left = jnp.concatenate([source[at, m], source[at + 1, m]], axis=1)
                z0 = 4 * (at % 4) + (residue ^ (2 * (at // 4) + step // 4))
                z1 = z0 + 4
                columns = [
                    jnp.concatenate([basis_ref[2 * pair + i, m, z0], basis_ref[2 * pair + i, m, z1]], axis=0) for i in range(2)
                ]
                right = jnp.concatenate(columns, axis=1)
                total = total + jnp.dot(left, right, preferred_element_type=f32)
            out_ref[2 * pair, m] = total[:, :128].astype(bf16)
            out_ref[2 * pair + 1, m] = total[:, 128:].astype(bf16)


def project(z, near, far, basis):
    return pl.pallas_call(
        project_kernel,
        out_shape=jax.ShapeDtypeStruct((X, 2, 256, 128), bf16),
        in_specs=[SCALAR] + [WHOLE] * 3,
        out_specs=WHOLE,
        compiler_params=PARAMS,
        cost_estimate=pl.CostEstimate(flops=4 * 256 * 2048 * 512, bytes_accessed=6800000, transcendentals=0),
        name="project",
    )(z, near, far, basis)


def scale_kernel(rows_ref, p0, p1, p2a, p2b, p3, out_ref):
    def block(j, at):
        if j == 2:
            return p2a[at] if at < 4 else p2b[at - 4]
        return {0: p0, 1: p1, 3: p3}[j][at]

    for j in range(4):
        for a in (0, 2):
            total = jnp.zeros((256, 256), f32)
            for h in range(2):
                right = jnp.concatenate([block(j, 4 * h + a), block(j, 4 * h + a + 1)], axis=1)
                total = total + jnp.dot(rows_ref[h], right, preferred_element_type=f32)
            at = (4 * j + a) * 128
            out_ref[:, :, at : at + 256] = total.reshape(32, 8, 256).astype(bf16)


def scale_part(rows, p0, p1, p2a, p2b, p3):
    return pl.pallas_call(
        scale_kernel,
        out_shape=jax.ShapeDtypeStruct((X * Y * C, 8, 2048), bf16),
        in_specs=[WHOLE] * 6,
        out_specs=WHOLE,
        compiler_params=PARAMS,
        cost_estimate=pl.CostEstimate(flops=2 * 256 * 512 * 2048, bytes_accessed=3300000, transcendentals=0),
        name="scale",
    )(rows, p0, p1, p2a, p2b, p3)


def exchange(value, axis):
    return lax.all_to_all(value, axis, split_axis=0, concat_axis=0, tiled=True)


def per_device(activations, out_grads, basis_in, basis_out, grad_eigen):
    tokens = activations.shape[0]
    ring = lax.axis_index(RING)
    z = (ring % 16).astype(jnp.int32).reshape(1)
    high = lax.axis_index("zh") == 1

    def mine(halves):
        return jnp.where(high, halves[1], halves[0])

    def theirs(halves):
        return jnp.where(high, halves[0], halves[1])

    def in_order(own, other):
        return jnp.stack([jnp.where(high, other, own), jnp.where(high, own, other)])

    bases = jnp.stack([basis_out.reshape(16, X, 128, 128), basis_in.reshape(16, X, 128, 128)])
    bases = exchange(bases.transpose(2, 0, 1, 3, 4), "x")

    have = lax.all_gather(jnp.stack([out_grads, activations]), ("z8", "z4"), axis=0, tiled=False)
    have = jnp.concatenate([have, swap(have, "z2")], axis=0)
    have, bases, grad_eigen = together(have, bases, grad_eigen)
    grad = grad_eigen.reshape(Y, ZH, C, 8, 512).transpose(0, 2, 1, 3, 4).reshape(Y * C, ZH, 8, 512)
    grad = exchange(grad, ("y", "c"))
    far, have, grad = together(swap(have, "z1"), have, grad)
    grad = grad.transpose(1, 0, 2, 3)

    part = project(z, have, far, bases)
    projected = jnp.sum(exchange(part, "x").astype(f32), axis=0)
    squares = (projected * projected).astype(bf16)
    squares_in = squares[1].T.reshape(Y, ZH, C * 8, tokens).transpose(1, 0, 2, 3).reshape(ZH, 64, tokens)

    sent = jnp.concatenate([theirs(squares_in), theirs(grad).reshape(64, 512)], axis=1)
    p0 = lax.all_gather(squares[0], ("zh", "z8", "z4"), axis=0, tiled=False)
    p0, got = together(p0, swap(sent, "zh"))
    rows_in = in_order(mine(squares_in), got[:, :tokens])
    rows_in = lax.all_gather(rows_in, "x", axis=0, tiled=False)
    rows_in = rows_in.reshape(X, ZH, Y, C, 8, tokens).transpose(1, 3, 2, 0, 4, 5).reshape(ZH, 256, tokens)
    grad = in_order(mine(grad), got[:, tokens:].reshape(Y * C, 8, 512))
    grad = grad.reshape(ZH, Y, C, 8, 512).transpose(3, 1, 0, 2, 4).reshape(8, 8192)
    p3, p1, rows_in = together(around(p0, 1), around(p0, -1), rows_in)
    p2a, p2b, grad = together(around(p1[:4], -1), around(p3[4:], 1), grad)

    partial = exchange(scale_part(rows_in, p0, p1, p2a, p2b, p3).reshape(C, Y * X, 8, 2048), "c")
    partial = exchange((partial[0].astype(f32) + partial[1].astype(f32)).astype(bf16), ("y", "x"))
    rows = jnp.sum(partial.reshape(Y, X, 8, 2048).astype(f32), axis=0).reshape(X, 8, 4, 4, 128)
    rows = rows.transpose(1, 3, 2, 0, 4)
    odd, two = (ring % 2) == 1, ((ring // 2) % 2) == 1
    rows = jnp.where(odd, jnp.roll(rows, 1, axis=2), rows)
    rows = jnp.where(two, jnp.roll(rows, 2, axis=2), rows)
    rows = rows.reshape(8, 8192)

    scaling = rows / (tokens * Y * ZH * C)
    return (grad.astype(f32) / (scaling + damping)).astype(bf16)


def solution(mesh):
    fine = Mesh(mesh.devices.reshape(Y, ZH, C, 2, 2, 2, 2, X), AXES)
    dp, mp = ("y", "zh", "c"), Z_BITS + ("x",)
    placed = (P(dp, mp), P(dp, mp), P(None, mp), P(None, mp), P(mp, dp))
    return jax.shard_map(
        per_device, mesh=fine, in_specs=placed, out_specs=P(mp + dp, None), check_vma=False
    )
```

```python
import jax
import jax.numpy as jnp
from jax import lax
from jax.experimental import pallas as pl
from jax.experimental.pallas import tpu as pltpu
from jax.sharding import Mesh, PartitionSpec as P

damping = 0.1
Y, ZH, C, X = 4, 2, 2, 4
Z_BITS = ("z8", "z4", "z2", "z1")
RING = ("zh",) + Z_BITS
AXES = ("y", "zh", "c") + Z_BITS + ("x",)
f32, bf16 = jnp.float32, jnp.bfloat16
PARAMS = pltpu.CompilerParams(vmem_limit_bytes=16 * 2**20)
SCALAR = pl.BlockSpec(memory_space=pltpu.SMEM)
WHOLE = pl.BlockSpec(memory_space=pltpu.VMEM)
def together(*values):
    return lax.optimization_barrier(values)


def swap(value, axis):
    return lax.ppermute(value, axis, [(0, 1), (1, 0)])


def around(value, hops):
    return lax.ppermute(value, RING, [(i, (i + hops) % 32) for i in range(32)])


def project_kernel(blocks_ref, basis_ref, out_ref):
    for m in range(2):
        for pair in range(2):
            total = jnp.zeros((256, 256), f32)
            for step in range(8):
                residue, at = step // 2, 2 * (step % 2)
                left = jnp.concatenate([blocks_ref[residue, at, m], blocks_ref[residue, at + 1, m]], axis=1)
                z = 4 * at + residue
                columns = [
                    jnp.concatenate([basis_ref[2 * pair + i, m, z], basis_ref[2 * pair + i, m, z + 4]], axis=0) for i in range(2)
                ]
                right = jnp.concatenate(columns, axis=1)
                total = total + jnp.dot(left, right, preferred_element_type=f32)
            out_ref[2 * pair, m] = total[:, :128].astype(bf16)
            out_ref[2 * pair + 1, m] = total[:, 128:].astype(bf16)


def project(blocks, basis):
    return pl.pallas_call(
        project_kernel,
        out_shape=jax.ShapeDtypeStruct((X, 2, 256, 128), bf16),
        in_specs=[WHOLE] * 2,
        out_specs=WHOLE,
        compiler_params=PARAMS,
        cost_estimate=pl.CostEstimate(flops=4 * 256 * 2048 * 512, bytes_accessed=6800000, transcendentals=0),
        name="project",
    )(blocks, basis)


def scale_kernel(rows_ref, p0, p1, p2a, p2b, p3, out_ref):
    def block(j, at):
        if j == 2:
            return p2a[at] if at < 4 else p2b[at - 4]
        return {0: p0, 1: p1, 3: p3}[j][at]

    for j in range(4):
        for a in (0, 2):
            total = jnp.zeros((256, 256), f32)
            for h in range(2):
                right = jnp.concatenate([block(j, 4 * h + a), block(j, 4 * h + a + 1)], axis=1)
                total = total + jnp.dot(rows_ref[h], right, preferred_element_type=f32)
            at = (4 * j + a) * 128
            out_ref[:, :, at : at + 256] = total.reshape(32, 8, 256).astype(bf16)


def scale_part(rows, p0, p1, p2a, p2b, p3):
    return pl.pallas_call(
        scale_kernel,
        out_shape=jax.ShapeDtypeStruct((X * Y * C, 8, 2048), bf16),
        in_specs=[WHOLE] * 6,
        out_specs=WHOLE,
        compiler_params=PARAMS,
        cost_estimate=pl.CostEstimate(flops=2 * 256 * 512 * 2048, bytes_accessed=3300000, transcendentals=0),
        name="scale",
    )(rows, p0, p1, p2a, p2b, p3)


def exchange(value, axis):
    return lax.all_to_all(value, axis, split_axis=0, concat_axis=0, tiled=True)


def per_device(activations, out_grads, basis_in, basis_out, grad_eigen):
    tokens = activations.shape[0]
    ring = lax.axis_index(RING)
    high = lax.axis_index("zh") == 1

    def mine(halves):
        return jnp.where(high, halves[1], halves[0])

    def theirs(halves):
        return jnp.where(high, halves[0], halves[1])

    def in_order(own, other):
        return jnp.stack([jnp.where(high, other, own), jnp.where(high, own, other)])

    bases = jnp.stack([basis_out.reshape(16, X, 128, 128), basis_in.reshape(16, X, 128, 128)])
    bases = exchange(bases.transpose(2, 0, 1, 3, 4), "x")

    have = lax.all_gather(jnp.stack([out_grads, activations]), ("z8", "z4"), axis=0, tiled=False)
    have, bases = together(have, bases)
    have = exchange(jnp.broadcast_to(have[None], (4,) + have.shape), ("z2", "z1"))
    grad = grad_eigen.reshape(Y, ZH, C, 8, 512).transpose(1, 0, 2, 3, 4)

    part = project(have, bases)
    projected = jnp.sum(exchange(part, "x").astype(f32), axis=0)
    squares = (projected * projected).astype(bf16)
    squares_in = squares[1].T.reshape(Y, ZH, C * 8, tokens).transpose(1, 0, 2, 3).reshape(ZH, 64, tokens)

    sent = jnp.concatenate([theirs(squares_in), theirs(grad).reshape(64, 512)], axis=1)
    p0 = lax.all_gather(squares[0], ("zh", "z8", "z4"), axis=0, tiled=False)
    p0, got = together(p0, swap(sent, "zh"))
    rows_in = in_order(mine(squares_in), got[:, :tokens])
    rows_in = lax.all_gather(rows_in, "x", axis=0, tiled=False)
    rows_in = rows_in.reshape(X, ZH, Y, C, 8, tokens).transpose(1, 3, 2, 0, 4, 5).reshape(ZH, 256, tokens)
    grad = in_order(mine(grad), got[:, tokens:].reshape(Y, C, 8, 512)).transpose(1, 2, 0, 3, 4).reshape(Y * C, ZH, 8, 512)
    grad = exchange(grad, ("y", "c")).reshape(Y, C, ZH, 8, 512).transpose(3, 0, 2, 1, 4).reshape(8, 8192)
    p3, p1, rows_in = together(around(p0, 1), around(p0, -1), rows_in)
    p2a, p2b, grad = together(around(p1[:4], -1), around(p3[4:], 1), grad)

    partial = exchange(scale_part(rows_in, p0, p1, p2a, p2b, p3).reshape(C, Y * X, 8, 2048), "c")
    partial = exchange((partial[0].astype(f32) + partial[1].astype(f32)).astype(bf16), ("y", "x"))
    rows = jnp.sum(partial.reshape(Y, X, 8, 2048).astype(f32), axis=0).reshape(X, 8, 4, 4, 128)
    rows = rows.transpose(1, 3, 2, 0, 4)
    odd, two = (ring % 2) == 1, ((ring // 2) % 2) == 1
    rows = jnp.where(odd, jnp.roll(rows, 1, axis=2), rows)
    rows = jnp.where(two, jnp.roll(rows, 2, axis=2), rows)
    rows = rows.reshape(8, 8192)

    scaling = rows / (tokens * Y * ZH * C)
    return (grad.astype(f32) / (scaling + damping)).astype(bf16)


def solution(mesh):
    fine = Mesh(mesh.devices.reshape(Y, ZH, C, 2, 2, 2, 2, X), AXES)
    dp, mp = ("y", "zh", "c"), Z_BITS + ("x",)
    placed = (P(dp, mp), P(dp, mp), P(None, mp), P(None, mp), P(mp, dp))
    return jax.shard_map(
        per_device, mesh=fine, in_specs=placed, out_specs=P(mp + dp, None), check_vma=False
    )
```

```python
import jax
import jax.numpy as jnp
from jax import lax
from jax.experimental import pallas as pl
from jax.experimental.pallas import tpu as pltpu
from jax.sharding import Mesh, PartitionSpec as P

damping = 0.1
Y, ZH, C, X = 4, 2, 2, 4
Z_BITS = ("z8", "z4", "z2", "z1")
RING = ("zh",) + Z_BITS
AXES = ("y", "zh", "c") + Z_BITS + ("x",)
f32, bf16 = jnp.float32, jnp.bfloat16
PARAMS = pltpu.CompilerParams(vmem_limit_bytes=16 * 2**20)
SCALAR = pl.BlockSpec(memory_space=pltpu.SMEM)
WHOLE = pl.BlockSpec(memory_space=pltpu.VMEM)
def together(*values):
    return lax.optimization_barrier(values)


def swap(value, axis):
    return lax.ppermute(value, axis, [(0, 1), (1, 0)])


def around(value, hops):
    return lax.ppermute(value, RING, [(i, (i + hops) % 32) for i in range(32)])


def project_kernel(z_ref, near_ref, far_ref, basis_ref, out_ref):
    residue = lax.rem(z_ref[0], 4)
    for m in range(2):
        for pair in range(2):
            total = jnp.zeros((256, 256), f32)
            for step in range(8):
                source = near_ref if step < 4 else far_ref
                at = 2 * (step % 4)
                left = jnp.concatenate([source[at, m], source[at + 1, m]], axis=1)
                z0 = 4 * (at % 4) + (residue ^ (2 * (at // 4) + step // 4))
                z1 = z0 + 4
                columns = [
                    jnp.concatenate([basis_ref[2 * pair + i, m, z0], basis_ref[2 * pair + i, m, z1]], axis=0) for i in range(2)
                ]
                right = jnp.concatenate(columns, axis=1)
                total = total + jnp.dot(left, right, preferred_element_type=f32)
            out_ref[2 * pair, m] = total[:, :128].astype(bf16)
            out_ref[2 * pair + 1, m] = total[:, 128:].astype(bf16)


def project(z, near, far, basis):
    return pl.pallas_call(
        project_kernel,
        out_shape=jax.ShapeDtypeStruct((X, 2, 256, 128), bf16),
        in_specs=[SCALAR] + [WHOLE] * 3,
        out_specs=WHOLE,
        compiler_params=PARAMS,
        cost_estimate=pl.CostEstimate(flops=4 * 256 * 2048 * 512, bytes_accessed=6800000, transcendentals=0),
        name="project",
    )(z, near, far, basis)


def scale_kernel(rows_ref, p0, p1, p2a, p2b, p3, out_ref):
    def block(j, at):
        if j == 2:
            return p2a[at] if at < 4 else p2b[at - 4]
        return {0: p0, 1: p1, 3: p3}[j][at]

    for j in range(4):
        for a in (0, 2):
            total = jnp.zeros((256, 256), f32)
            for h in range(2):
                right = jnp.concatenate([block(j, 4 * h + a), block(j, 4 * h + a + 1)], axis=1)
                total = total + jnp.dot(rows_ref[h], right, preferred_element_type=f32)
            at = (4 * j + a) * 128
            out_ref[:, :, at : at + 256] = total.reshape(32, 8, 256).astype(bf16)


def scale_part(rows, p0, p1, p2a, p2b, p3):
    return pl.pallas_call(
        scale_kernel,
        out_shape=jax.ShapeDtypeStruct((X * Y * C, 8, 2048), bf16),
        in_specs=[WHOLE] * 6,
        out_specs=WHOLE,
        compiler_params=PARAMS,
        cost_estimate=pl.CostEstimate(flops=2 * 256 * 512 * 2048, bytes_accessed=3300000, transcendentals=0),
        name="scale",
    )(rows, p0, p1, p2a, p2b, p3)


def exchange(value, axis):
    return lax.all_to_all(value, axis, split_axis=0, concat_axis=0, tiled=True)


def per_device(activations, out_grads, basis_in, basis_out, grad_eigen):
    tokens = activations.shape[0]
    ring = lax.axis_index(RING)
    z = (ring % 16).astype(jnp.int32).reshape(1)
    high = lax.axis_index("zh") == 1

    def mine(halves):
        return jnp.where(high, halves[1], halves[0])

    def theirs(halves):
        return jnp.where(high, halves[0], halves[1])

    def in_order(own, other):
        return jnp.stack([jnp.where(high, other, own), jnp.where(high, own, other)])

    bases = jnp.stack([basis_out.reshape(16, X, 128, 128), basis_in.reshape(16, X, 128, 128)])
    bases = exchange(bases.transpose(2, 0, 1, 3, 4), "x")

    have = lax.all_gather(jnp.stack([out_grads, activations]), ("z8", "z4"), axis=0, tiled=False)
    have = jnp.concatenate([have, swap(have, "z2")], axis=0)
    have, bases, grad_eigen = together(have, bases, grad_eigen)
    grad = grad_eigen.reshape(Y, ZH, C, 8, 512).transpose(0, 2, 1, 3, 4).reshape(Y * C, ZH, 8, 512)
    grad = exchange(grad, ("y", "c"))
    far, have, grad = together(swap(have, "z1"), have, grad)
    grad = grad.transpose(1, 0, 2, 3)

    part = project(z, have, far, bases)
    projected = jnp.sum(exchange(part, "x").astype(f32), axis=0)
    squares = (projected * projected).astype(bf16)
    squares_in = squares[1].T.reshape(Y, ZH, C * 8, tokens).transpose(1, 0, 2, 3).reshape(ZH, 64, tokens)

    sent = jnp.concatenate([theirs(squares_in), theirs(grad).reshape(64, 512)], axis=1)
    p0 = lax.all_gather(squares[0], ("zh", "z8", "z4"), axis=0, tiled=False)
    p0, sent = together(p0, sent)
    p3, p1, got = together(around(p0, 1), around(p0, -1), swap(sent, "zh"))
    p2a, p2b = around(p1[:4], -1), around(p3[4:], 1)
    rows_in = in_order(mine(squares_in), got[:, :tokens])
    rows_in = lax.all_gather(rows_in, "x", axis=0, tiled=False)
    rows_in = rows_in.reshape(X, ZH, Y, C, 8, tokens).transpose(1, 3, 2, 0, 4, 5).reshape(ZH, 256, tokens)
    grad = in_order(mine(grad), got[:, tokens:].reshape(Y * C, 8, 512))
    grad = grad.reshape(ZH, Y, C, 8, 512).transpose(3, 1, 0, 2, 4).reshape(8, 8192)
    p2a, p2b, grad, rows_in = together(p2a, p2b, grad, rows_in)

    partial = exchange(scale_part(rows_in, p0, p1, p2a, p2b, p3).reshape(C, Y * X, 8, 2048), "c")
    partial = exchange((partial[0].astype(f32) + partial[1].astype(f32)).astype(bf16), ("y", "x"))
    rows = jnp.sum(partial.reshape(Y, X, 8, 2048).astype(f32), axis=0).reshape(X, 8, 4, 4, 128)
    rows = rows.transpose(1, 3, 2, 0, 4)
    odd, two = (ring % 2) == 1, ((ring // 2) % 2) == 1
    rows = jnp.where(odd, jnp.roll(rows, 1, axis=2), rows)
    rows = jnp.where(two, jnp.roll(rows, 2, axis=2), rows)
    rows = rows.reshape(8, 8192)

    scaling = rows / (tokens * Y * ZH * C)
    return (grad.astype(f32) / (scaling + damping)).astype(bf16)


def solution(mesh):
    fine = Mesh(mesh.devices.reshape(Y, ZH, C, 2, 2, 2, 2, X), AXES)
    dp, mp = ("y", "zh", "c"), Z_BITS + ("x",)
    placed = (P(dp, mp), P(dp, mp), P(None, mp), P(None, mp), P(mp, dp))
    return jax.shard_map(
        per_device, mesh=fine, in_specs=placed, out_specs=P(mp + dp, None), check_vma=False
    )
```
